32 devices in a mesh: ta: 16 (over z, y, x), gz: 2 (over core).
Axes of the slice: x: 2, y: 2, z: 4, core: 2. Of those that a mesh axis runs over, the one named last changes fastest.
Arguments:
- propagator: float32 [2, 12, 12, 16, 13824], P(None, None, None, 'ta', 'gz'), may hold values from -6 to 6
- backward: float32 [2, 12, 12, 16, 13824], P(None, None, None, 'ta', 'gz'), may hold values from -6 to 6
- sink_time: int32 [1], replicated, may hold values from 0 to 15
- source_position: int32 [3], replicated, may hold values from 0 to 23
- momenta: int32 [27, 3], replicated, may hold values from -3 to 3
- gamma_table: int32 [16], replicated, may hold values from 0 to 15, each once
Outputs:
- correlator: float32 [2, 16, 16, 27], P(None, 'ta', 'gz')
The draws below stay inside these ranges and needn't reach their ends.
Inputs may be any that keep to these rules, and one draw needn't show every extreme that they name: `gamma_table`: each of 0 to 15 appears exactly once.
All inputs are finite; a program needn't handle non-finite values.
Results may differ from the reference program's by a relative error of at most 0.00007.
Values sent between devices are 32-bit elements; how exact they have to be, the bound alone decides.
A program may use at most 192 MiB of HBM per device.

```python
import math
import jax
import jax.numpy as jnp
import numpy as np
from jax import lax

L = 24
NG = 16
NP = 27
T_SIZE = 16
V3 = 13824


def place_ends(drawn, stream_key, smallest, largest):
    shape = drawn.shape
    place = [jax.random.randint(jax.random.fold_in(stream_key, axis), (), 0, shape[axis]) for axis in range(len(shape))]
    drawn = drawn.at[tuple(place)].set(smallest)
    longest = shape.index(max(shape))
    place[longest] = (place[longest] + 1) % shape[longest]
    return drawn.at[tuple(place)].set(largest)


def steps_of(rng, extent, cuts, low, top_value):
    loudness, own = 1.0, jax.random.fold_in(rng, 6)
    for position, shards_of in cuts:
        heights = jnp.exp(jax.random.uniform(jax.random.fold_in(own, position), (shards_of,), jnp.float32, low / len(cuts), top_value / len(cuts)))
        loudness = loudness * jnp.repeat(heights, extent[position] // shards_of).reshape([-1 if axis == position else 1 for axis in range(len(extent))])
    return loudness


def scatter_about(own_key, shape, scale, most, shards=(), kind=jnp.bfloat16):
    gain = steps_of(own_key, shape, shards, -0.22, 0.18) if shards else 1.0
    values = jax.random.normal(own_key, shape, jnp.float32) * scale * gain
    return jnp.minimum(jnp.maximum(values, -most), most).astype(kind)


def setup_inputs(seed: int = 0) -> dict:
    seeds = jax.random.split(jax.random.key(seed), 7)
    return {
        "propagator": scatter_about(seeds[0], (2, 12, 12, T_SIZE, V3), 1.0, 6.0, ((3, 16), (4, 2)), jnp.float32),
        "backward": scatter_about(seeds[1], (2, 12, 12, T_SIZE, V3), 1.0, 6.0, ((3, 16), (4, 2)), jnp.float32),
        "sink_time": jax.random.randint(seeds[2], (1,), 0, T_SIZE).astype(jnp.int32),
        "source_position": jax.random.randint(seeds[3], (3,), 0, L).astype(jnp.int32),
        "momenta": place_ends(jax.random.randint(seeds[4], (NP, 3), -3, 4), jax.random.fold_in(seeds[4], 1), -3, 3).astype(jnp.int32),
        "gamma_table": jax.random.permutation(seeds[5], NG).astype(jnp.int32),
    }


def gamma_tables():
    paulis = [np.eye(2), np.array([[0.0, 1.0], [1.0, 0.0]]), np.array([[0.0, -1j], [1j, 0.0]]), np.array([[1.0, 0.0], [0.0, -1.0]])]
    matrices = np.stack([np.kron(paulis[number // 4], paulis[number % 4]) for number in range(16)])
    return np.stack([matrices.real, matrices.imag]).astype(np.float32)

def complex_product(einsum_form, left_term, right_term):

    def product(first_op, second_op):
        return jnp.einsum(einsum_form, first_op, second_op, precision=lax.Precision.HIGHEST)
    real_part = product(left_term[0], right_term[0]) - product(left_term[1], right_term[1])
    imag_part = product(left_term[0], right_term[1]) + product(left_term[1], right_term[0])
    return jnp.stack([real_part, imag_part])

def complex_reduce(left_term, right_term, reduce_axis):
    real_part = lax.optimization_barrier(jnp.sum(left_term[0] * right_term[0] - left_term[1] * right_term[1], axis=reduce_axis))
    imag_part = lax.optimization_barrier(jnp.sum(left_term[0] * right_term[1] + left_term[1] * right_term[0], axis=reduce_axis))
    return jnp.stack([real_part, imag_part])

def conjugate(values):
    return jnp.stack([values[0], -values[1]])

def source_field(sink_slice):
    return 0.125 * complex_reduce(sink_slice[:, :, None, :, :], sink_slice[:, None, :, :, :], 2)

def phase_table(site_index, source_position, momenta):
    zplane = site_index // (L * L)
    xline = site_index // L % L
    yline = site_index % L
    wave = momenta[:, 0:1] * (xline[None, :] - source_position[0]) + momenta[:, 1:2] * (yline[None, :] - source_position[1]) + momenta[:, 2:3] * (zplane[None, :] - source_position[2])
    wave = jnp.mod(wave, L)
    angle_value = wave.astype(jnp.float32) * (2.0 * math.pi / L)
    return jnp.stack([jnp.cos(angle_value), -jnp.sin(angle_value)])

def slice_correlator(forward, back_field, sink_field, phases, gammas):
    site_count = forward.shape[-1]
    bound = complex_reduce(back_field[:, :, :, None, :], sink_field[:, None, :, :, :], 1)
    forward_split = forward.reshape(2, 4, 36, site_count)
    bound_split = conjugate(bound).reshape(2, 4, 36, site_count)
    spin_block = complex_reduce(forward_split[:, :, None, :, :], bound_split[:, None, :, :, :], 2)
    gamma_flat = jnp.transpose(gammas, (0, 1, 3, 2)).reshape(2, 16, 16)
    currents = complex_product('gb,bs->gs', gamma_flat, spin_block.reshape(2, 16, site_count))
    scale_factor = 1.0 / (72.0 * math.sqrt(L * L * L))
    return scale_factor * complex_product('gs,ps->gp', currents, phases)

def select_currents(gamma_table, values):
    onehot = (gamma_table[:, None] == jnp.arange(NG, dtype=jnp.int32)[None, :]).astype(jnp.float32)
    return jnp.einsum('cg,xgp->xcp', onehot, values, precision=lax.Precision.HIGHEST)

def reference(propagator, backward, sink_time, source_position, momenta, gamma_table):
    gammas = jnp.asarray(gamma_tables())
    sink_slice = lax.dynamic_index_in_dim(propagator, sink_time[0], 3, keepdims=False)
    sink_field = source_field(sink_slice)
    phases = phase_table(jnp.arange(L * L * L, dtype=jnp.int32), source_position, momenta)

    def one_slice(slice_index):
        forward = lax.dynamic_index_in_dim(propagator, slice_index, 3, keepdims=False)
        back_field = lax.dynamic_index_in_dim(backward, slice_index, 3, keepdims=False)
        return select_currents(gamma_table, slice_correlator(forward, back_field, sink_field, phases, gammas))
    stacked = lax.map(one_slice, jnp.arange(T_SIZE, dtype=jnp.int32))
    return jnp.transpose(stacked, (1, 0, 2, 3))
```

```python
import math

import jax
import jax.numpy as jnp
import numpy as np
from jax import lax
from jax.experimental import pallas as pl
from jax.experimental.pallas import tpu as pltpu
from jax.sharding import PartitionSpec as P

L = 24
NG = 16


def gamma_tables():
    paulis = [
        np.eye(2),
        np.array([[0.0, 1.0], [1.0, 0.0]]),
        np.array([[0.0, -1j], [1j, 0.0]]),
        np.array([[1.0, 0.0], [0.0, -1.0]]),
    ]
    matrices = np.stack([np.kron(paulis[number // 4], paulis[number % 4]) for number in range(16)])
    return np.stack([matrices.real, matrices.imag]).astype(np.float32)


def complex_product(einsum_form, left_term, right_term):

    def product(first_op, second_op):
        return jnp.einsum(einsum_form, first_op, second_op, precision=lax.Precision.HIGHEST)

    real_part = product(left_term[0], right_term[0]) - product(left_term[1], right_term[1])
    imag_part = product(left_term[0], right_term[1]) + product(left_term[1], right_term[0])
    return jnp.stack([real_part, imag_part])


LANES = 128
SUBLANES = 8
PAIRS = [(row, column) for row in range(12) for column in range(row, 12)]
PAIR_NUMBER = {pair: number for number, pair in enumerate(PAIRS)}


def multiply_add(total, left, right):
    real = left[0] * right[0] - left[1] * right[1]
    imag = left[0] * right[1] + left[1] * right[0]
    return (real, imag) if total is None else (total[0] + real, total[1] + imag)


def multiply_add_conj(total, left, right):
    real = left[0] * right[0] + left[1] * right[1]
    imag = left[1] * right[0] - left[0] * right[1]
    return (real, imag) if total is None else (total[0] + real, total[1] + imag)


def sink_kernel(owned_ref, s_ref, sigma_ref):
    owned = owned_ref[0] == 1

    @pl.when(owned)
    def _():
        for row in range(12):
            left = [(s_ref[row * 12 + m], s_ref[144 + row * 12 + m]) for m in range(12)]
            for column in range(row, 12):
                total = None
                for m in range(12):
                    right = (s_ref[column * 12 + m], s_ref[144 + column * 12 + m])
                    total = multiply_add(total, left[m], right)
                number = PAIR_NUMBER[row, column]
                sigma_ref[number] = 0.125 * total[0]
                sigma_ref[len(PAIRS) + number] = 0.125 * total[1]

    @pl.when(jnp.logical_not(owned))
    def _():
        sigma_ref[...] = jnp.zeros_like(sigma_ref)


def spin_kernel(s_ref, h_ref, sigma_ref, m_ref):
    def one_spin(alpha, carry):
        sums = [None] * 4
        for color in range(3):
            base = (alpha * 3 + color) * 12
            h_row = [(h_ref[base + m], h_ref[144 + base + m]) for m in range(12)]
            b_row = []
            for k in range(12):
                total = None
                for m in range(12):
                    number = PAIR_NUMBER[min(m, k), max(m, k)]
                    sigma = (sigma_ref[number], sigma_ref[len(PAIRS) + number])
                    total = multiply_add(total, h_row[m], sigma)
                b_row.append(total)
            for beta in range(4):
                start = (beta * 3 + color) * 12
                for m in range(12):
                    forward = (s_ref[start + m], s_ref[144 + start + m])
                    sums[beta] = multiply_add_conj(sums[beta], forward, b_row[m])
        for beta in range(4):
            m_ref[beta * 4 + alpha] = sums[beta][0]
            m_ref[16 + beta * 4 + alpha] = sums[beta][1]
        return carry

    lax.fori_loop(0, 4, one_spin, 0)


def site_block(rows):
    return pl.BlockSpec((rows, SUBLANES, LANES), lambda step: (0, step, 0))


def sink_source(owned, sites):
    rows = sites.shape[1]
    return pl.pallas_call(
        sink_kernel,
        grid=(pl.cdiv(rows, SUBLANES),),
        in_specs=[pl.BlockSpec(memory_space=pltpu.SMEM), site_block(288)],
        out_specs=site_block(2 * len(PAIRS)),
        out_shape=jax.ShapeDtypeStruct((2 * len(PAIRS), rows, LANES), jnp.float32),
        name="sink_source",
    )(owned, sites)


def spin_blocks(forward, back_field, sigma):
    rows = forward.shape[1]
    return pl.pallas_call(
        spin_kernel,
        grid=(pl.cdiv(rows, SUBLANES),),
        in_specs=[site_block(288), site_block(288), site_block(2 * len(PAIRS))],
        out_specs=site_block(32),
        out_shape=jax.ShapeDtypeStruct((32, rows, LANES), jnp.float32),
        name="spin_blocks",
    )(forward, back_field, sigma)


def tiles(field):
    local_times, site_count = field.shape[3:]
    flat = field.reshape(288, local_times, site_count // LANES, LANES)
    return [flat[:, time] for time in range(local_times)]


def phase_table(site_index, source_position, momenta):
    zplane = site_index // (L * L)
    xline = site_index // L % L
    yline = site_index % L
    wave = (
        momenta[:, 0:1] * (xline[None, :] - source_position[0])
        + momenta[:, 1:2] * (yline[None, :] - source_position[1])
        + momenta[:, 2:3] * (zplane[None, :] - source_position[2])
    )
    wave = jnp.mod(wave, L)
    angle_value = wave.astype(jnp.float32) * (2.0 * math.pi / L)
    return jnp.stack([jnp.cos(angle_value), -jnp.sin(angle_value)])


def select_currents(gamma_table, values):
    onehot = (gamma_table[:, None] == jnp.arange(NG, dtype=jnp.int32)[None, :]).astype(jnp.float32)
    return jnp.einsum("cg,xgp->xcp", onehot, values, precision=lax.Precision.HIGHEST)


def body(propagator, backward, sink_time, source_position, momenta, gamma_table):
    gamma_flat = jnp.asarray(np.transpose(gamma_tables(), (0, 1, 3, 2)).reshape(2, 16, 16))
    local_times = propagator.shape[3]
    site_count = propagator.shape[4]
    local_time = sink_time[0] - lax.axis_index("ta") * local_times
    owned = jnp.logical_and(local_time >= 0, local_time < local_times)
    local_index = jnp.clip(local_time, 0, local_times - 1)
    forwards, backwards = tiles(propagator), tiles(backward)
    sink_slice = forwards[0]
    for time in range(1, local_times):
        sink_slice = jnp.where(local_index == time, forwards[time], sink_slice)
    sigma = lax.psum(sink_source(owned.astype(jnp.int32)[None], sink_slice), "ta")
    first_site = lax.axis_index("gz") * site_count
    phases = phase_table(
        first_site + jnp.arange(site_count, dtype=jnp.int32), source_position, momenta
    )
    momentum_count = momenta.shape[0]
    phase_rows = phases.reshape(2 * momentum_count, site_count)
    scale_factor = 1.0 / (72.0 * math.sqrt(L * L * L))
    stacked = []
    for time in range(local_times):
        spin = spin_blocks(forwards[time], backwards[time], sigma)
        sums = jnp.einsum(
            "bs,ps->bp",
            spin.reshape(32, site_count),
            phase_rows,
            precision=lax.Precision.HIGHEST,
        ).reshape(2, 16, 2, momentum_count)
        real = sums[0, :, 0] - sums[1, :, 1]
        imag = sums[0, :, 1] + sums[1, :, 0]
        currents = complex_product("gb,bp->gp", gamma_flat, jnp.stack([real, imag]))
        stacked.append(select_currents(gamma_table, scale_factor * currents))
    local_sums = jnp.stack(stacked, axis=1)
    return lax.psum_scatter(local_sums, "gz", scatter_dimension=2, tiled=True)


def solution(mesh):
    in_specs = (
        P(None, None, None, "ta", "gz"),
        P(None, None, None, "ta", "gz"),
        P(),
        P(),
        P(),
        P(),
    )
    out_specs = P(None, "ta", "gz", None)
    return jax.shard_map(body, mesh=mesh, in_specs=in_specs, out_specs=out_specs, check_vma=False)
```
